32 devices in a mesh: dp: 16 (over z, y, core), tensor: 2 (over x).
Axes of the slice: x: 2, y: 2, z: 4, core: 2. Of those that a mesh axis runs over, the one named last changes fastest.
Arguments:
- hidden: float32 [4096, 1024], P(('dp', 'tensor')), may hold values from -6 to 6
- seg_ids: int32 [4096], P('dp'), may hold values from 0 to 4, as said below
- norm_gain: float32 [2, 1024], replicated, may hold values from 0.5 to 1.5
- weight_z: bfloat16 [2, 1024, 2048], P(None, 'dp', 'tensor'), may hold values from -0.1875 to 0.1875
- weight_x: bfloat16 [2, 1024, 2048], P(None, 'dp', 'tensor'), may hold values from -0.1875 to 0.1875
- weight_bc: bfloat16 [2, 1024, 256], P(None, ('dp', 'tensor')), may hold values from -0.1875 to 0.1875
- weight_dt: bfloat16 [2, 1024, 32], P(None, 'dp', 'tensor'), may hold values from -0.1875 to 0.1875
- taps_x: float32 [2, 5, 2048], P(None, None, 'tensor'), may hold values from -0.5 to 0.5
- taps_bc: float32 [2, 5, 256], replicated, may hold values from -0.5 to 0.5
- dt_bias: float32 [2, 32], P(None, 'tensor'), may hold values from -6 to -2.5
- decay_log: float32 [2, 32], P(None, 'tensor'), may hold values from 0 to 2.77
- skip_gain: float32 [2, 32], P(None, 'tensor'), may hold values from 0.5 to 1.5
- gate_gain: float32 [2, 2048], P(None, 'tensor'), may hold values from 0.5 to 1.5
- weight_out: bfloat16 [2, 2048, 1024], P(None, 'tensor', 'dp'), may hold values from -0.125 to 0.125
- cotangent: float32 [4096, 1024], P(('dp', 'tensor')), may hold values from -6 to 6
Outputs:
- block_out: float32 [4096, 1024], P(('dp', 'tensor'))
- grad_hidden: float32 [4096, 1024], P(('dp', 'tensor'))
- grad_norm_gain: float32 [2, 1024], replicated
- grad_weight_z: float32 [2, 1024, 2048], P(None, 'dp', 'tensor')
- grad_weight_x: float32 [2, 1024, 2048], P(None, 'dp', 'tensor')
- grad_weight_bc: float32 [2, 1024, 256], P(None, ('dp', 'tensor'))
- grad_weight_dt: float32 [2, 1024, 32], P(None, 'dp', 'tensor')
- grad_taps_x: float32 [2, 5, 2048], P(None, None, 'tensor')
- grad_taps_bc: float32 [2, 5, 256], replicated
- grad_dt_bias: float32 [2, 32], P(None, 'tensor')
- grad_decay_log: float32 [2, 32], P(None, 'tensor')
- grad_skip_gain: float32 [2, 32], P(None, 'tensor')
- grad_gate_gain: float32 [2, 2048], P(None, 'tensor')
- grad_weight_out: float32 [2, 2048, 1024], P(None, 'tensor', 'dp')
The draws below stay inside these ranges and needn't reach their ends.
Inputs may be any that keep to these rules, and one draw needn't show every extreme that they name: `seg_ids`: each pack of 256 positions numbers its sequences 0, 1, 2, ... in order from its first position and holds exactly 5 sequences; no sequence crosses a pack, every sequence has 1 to 128 positions, and every pack holds one of exactly 128.
All inputs are finite; a program needn't handle non-finite values.
Results may differ from the reference program's by a relative error of at most 0.017.
Values may be sent and summed in bfloat16 or wider, within the bound.
No kernel may reach another device: no remote copies, remote signals or barrier semaphores. Data moves between devices by JAX's collectives and lax.ppermute only.
A program may use at most 128 MiB of HBM per device.

```python
import jax
import jax.numpy as jnp
from jax import lax

D = 1024
HEADS = 32
INNER = 2048
STATE = 128
CONV = 4
SPAN = 256
LAYERS = 2
TOK_DEV = 256
SEQ_MAX = 128
TOKENS = 4096
N_TENSOR = 2


def draw_seg_ids(key, part):
    packs = TOKENS // TOK_DEV
    extra = max(2, TOK_DEV // 128)
    key_offset, key_score = jax.random.split(key)
    offset = jax.random.randint(key_offset, (packs, 1), 1, TOK_DEV - SEQ_MAX)
    position = jnp.arange(TOK_DEV, dtype=jnp.int32)[None, :]
    outside = ((position < offset) | (position > offset + SEQ_MAX)) & (position > 0)
    score = jax.random.randint(key_score, (packs, TOK_DEV), 0, TOK_DEV) * TOK_DEV + position
    masked = jnp.where(outside, score, TOK_DEV * TOK_DEV + position)
    threshold = jnp.sort(masked, axis=1)[:, extra - 1:extra]
    flagged = outside & (masked <= threshold)
    starts = (position == 0) | (position == offset) | (position == offset + SEQ_MAX) | flagged
    return (jnp.cumsum(starts.astype(jnp.int32), axis=1) - 1).reshape(TOKENS).astype(jnp.int32)


def shard_levels(own_key, dims, cuts, least, largest):
    level = 1.0
    for axis_at, parts in cuts:
        heights = jax.random.uniform(jax.random.fold_in(jax.random.fold_in(own_key, 6), axis_at), (parts,), jnp.float32, least / len(cuts), largest / len(cuts))
        level = level * jnp.repeat(jnp.exp(heights), dims[axis_at] // parts).reshape((-1,) + (1,) * (len(dims) - 1 - axis_at))
    return level


def scatter_about(own_key, extent, scale, limit, cuts=(), held_as=jnp.bfloat16):
    values = scale * jax.random.normal(own_key, extent, jnp.float32)
    if cuts:
        values = values * shard_levels(own_key, extent, cuts, -0.22, 0.18)
    return jnp.clip(values, -limit, limit).astype(held_as)


def setup_inputs(seed: int = 0) -> dict:
    key_list = jax.random.split(jax.random.key(seed), 16)
    hidden = scatter_about(key_list[0], (TOKENS, D), 1.0, 6.0, ((0, 32),), jnp.float32)
    seg_ids = draw_seg_ids(jax.random.fold_in(key_list[15], 71), 0)
    norm_gain = jnp.clip(1.0 + 0.1 * jax.random.normal(key_list[2], (LAYERS, D), jnp.float32), 0.5, 1.5)
    weight_z = scatter_about(key_list[3], (LAYERS, D, INNER), D ** -0.5, 0.1875, ((1, 16), (2, 2)))
    weight_x = scatter_about(key_list[4], (LAYERS, D, INNER), D ** -0.5, 0.1875, ((1, 16), (2, 2)))
    weight_bc = scatter_about(key_list[5], (LAYERS, D, 2 * STATE), D ** -0.5, 0.1875, ((1, 32),))
    weight_dt = scatter_about(key_list[6], (LAYERS, D, HEADS), D ** -0.5, 0.1875, ((1, 16), (2, 2)))
    taps_x = jnp.clip(jax.random.uniform(key_list[7], (LAYERS, CONV + 1, INNER), jnp.float32, -0.5, 0.5) * shard_levels(key_list[7], (LAYERS, CONV + 1, INNER), ((2, 2),), -0.4, 0.0), -0.5, 0.5)
    taps_bc = jnp.clip(jax.random.uniform(key_list[8], (LAYERS, CONV + 1, 2 * STATE), jnp.float32, -0.5, 0.5), -0.5, 0.5)
    dt_bias = jnp.clip(-6.0 + 3.5 * jax.random.uniform(key_list[9], (LAYERS, HEADS), jnp.float32) ** shard_levels(key_list[9], (LAYERS, HEADS), ((1, 2),), -0.2, 0.2), -6.0, -2.5)
    decay_log = jnp.clip(2.77 * jax.random.uniform(key_list[10], (LAYERS, HEADS), jnp.float32) ** shard_levels(key_list[10], (LAYERS, HEADS), ((1, 2),), -0.2, 0.2), 0.0, 2.77)
    skip_gain = jnp.clip(0.5 + 1.0 * jax.random.uniform(key_list[11], (LAYERS, HEADS), jnp.float32) ** shard_levels(key_list[11], (LAYERS, HEADS), ((1, 2),), -0.2, 0.2), 0.5, 1.5)
    gate_gain = jnp.clip(1.0 + 0.1 * jax.random.normal(key_list[12], (LAYERS, INNER), jnp.float32), 0.5, 1.5)
    weight_out = scatter_about(key_list[13], (LAYERS, INNER, D), INNER ** -0.5, 0.125, ((1, 2), (2, 16)))
    cotangent = scatter_about(key_list[14], (TOKENS, D), 1.0, 6.0, ((0, 32),), jnp.float32)
    return dict(hidden=hidden, seg_ids=seg_ids, norm_gain=norm_gain, weight_z=weight_z, weight_x=weight_x, weight_bc=weight_bc, weight_dt=weight_dt, taps_x=taps_x, taps_bc=taps_bc, dt_bias=dt_bias, decay_log=decay_log, skip_gain=skip_gain, gate_gain=gate_gain, weight_out=weight_out, cotangent=cotangent)


epsilon = 1e-05
contract_rows = (((0,), (0,)), ((), ()))
contract_cols = (((1,), (1,)), ((), ()))

def rms_norm(values, gain):
    return values * lax.rsqrt(lax.optimization_barrier(jnp.mean(values * values, axis=-1, keepdims=True)) + epsilon) * gain

def causal_conv(signal, taps, seg_ids):
    length = signal.shape[0]
    width = taps.shape[0] - 1
    total = taps[width] + taps[width - 1] * signal
    for shift in range(1, width):
        moved = jnp.concatenate([jnp.zeros((shift, signal.shape[1]), signal.dtype), signal[:length - shift]], axis=0)
        before = jnp.concatenate([jnp.full((shift,), -1, jnp.int32), seg_ids[:length - shift].astype(jnp.int32)], axis=0)
        total = total + taps[width - 1 - shift] * jnp.where((before == seg_ids)[:, None], moved, 0.0)
    return total

def span_scan(inputs, rates, b_proj, c_proj, seg_ids):
    tokens, heads, width = inputs.shape
    states = b_proj.shape[1]
    blocks = tokens // SPAN
    highest = lax.Precision.HIGHEST
    lower = jnp.arange(SPAN)[:, None] >= jnp.arange(SPAN)[None, :]

    def advance(carry, block):
        state, last = carry
        values_in, rate_block, b_block, c_block, seg_block = block
        cumulative = jnp.cumsum(rate_block, axis=0)
        same = (seg_block[:, None] == seg_block[None, :]) & lower
        gaps = cumulative[:, None, :] - cumulative[None, :, :]
        decay = jnp.exp(jnp.where(same[:, :, None], gaps, -jnp.inf))
        scores = jnp.dot(c_block, b_block.T, precision=highest)
        result = jnp.einsum('tsh,shp->thp', decay * scores[:, :, None], values_in, precision=highest)
        inside = (seg_block == last).astype(cumulative.dtype)
        entering = jnp.exp(cumulative) * inside[:, None]
        result = result + entering[:, :, None] * jnp.einsum('tn,hpn->thp', c_block, state, precision=highest)
        tail = seg_block[SPAN - 1]
        keep_weight = jnp.exp(jnp.where((seg_block == tail)[:, None], cumulative[SPAN - 1][None, :] - cumulative, -jnp.inf))
        carried = jnp.where(tail == last, jnp.exp(cumulative[SPAN - 1]), 0.0)
        fresh = jnp.einsum('sh,shp,sn->hpn', keep_weight, values_in, b_block, precision=highest)
        return ((carried[:, None, None] * state + fresh, tail), result)
    start = (jnp.zeros((heads, width, states), inputs.dtype), jnp.array(-1, jnp.int32))
    _, outputs = lax.scan(advance, start, (inputs.reshape(blocks, SPAN, heads, width), rates.reshape(blocks, SPAN, heads), b_proj.reshape(blocks, SPAN, states), c_proj.reshape(blocks, SPAN, states), seg_ids.reshape(blocks, SPAN)))
    return outputs.reshape(tokens, heads, width)

def mixer_group(proj_z, proj_x, proj_bc, proj_dt, taps_x, taps_bc, dt_bias, decay_log, skip_gain, gate_gain, seg_ids):
    tokens = proj_x.shape[0]
    heads = proj_dt.shape[1]
    width = proj_x.shape[1] // heads
    states = proj_bc.shape[1] // 2
    values = jax.nn.silu(causal_conv(proj_x, taps_x, seg_ids)).reshape(tokens, heads, width)
    b_and_c = jax.nn.silu(causal_conv(proj_bc, taps_bc, seg_ids))
    step_size = jax.nn.softplus(proj_dt + dt_bias)
    rates = -step_size * jnp.exp(decay_log)
    scanned = span_scan(values * step_size[:, :, None], rates, b_and_c[:, :states], b_and_c[:, states:], seg_ids)
    output = (scanned + skip_gain[None, :, None] * values).reshape(tokens, heads * width)
    gated = output * jax.nn.silu(proj_z)
    return gated * lax.rsqrt(lax.optimization_barrier(jnp.mean(gated * gated, axis=-1, keepdims=True)) + epsilon) * gate_gain
grouped_mixer = jax.vmap(mixer_group, in_axes=(0, 0, 0, 0, 0, 0, 0, 0, 0, 0, None))

def split_groups(matrix):
    leading, channels = matrix.shape
    return matrix.reshape(leading, N_TENSOR, channels // N_TENSOR).transpose(1, 0, 2)

def join_groups(stacked):
    groups, leading, channels = stacked.shape
    return stacked.transpose(1, 0, 2).reshape(leading, groups * channels)

def mixer_inputs(rows, weights):
    norm_gain, weight_z, weight_x, weight_bc, weight_dt, taps_x, taps_bc, dt_bias, decay_log, skip_gain, gate_gain, weight_out = weights
    normed = rms_norm(rows, norm_gain).astype(jnp.bfloat16)
    proj_z = jnp.dot(normed, weight_z, preferred_element_type=jnp.float32)
    proj_x = jnp.dot(normed, weight_x, preferred_element_type=jnp.float32)
    proj_bc = jnp.dot(normed, weight_bc, preferred_element_type=jnp.float32)
    proj_dt = jnp.dot(normed, weight_dt, preferred_element_type=jnp.float32)
    grouped = (split_groups(proj_z), split_groups(proj_x), jnp.broadcast_to(proj_bc, (N_TENSOR,) + proj_bc.shape), split_groups(proj_dt), split_groups(taps_x), jnp.broadcast_to(taps_bc, (N_TENSOR,) + taps_bc.shape), dt_bias.reshape(N_TENSOR, -1), decay_log.reshape(N_TENSOR, -1), skip_gain.reshape(N_TENSOR, -1), gate_gain.reshape(N_TENSOR, -1))
    return (normed, grouped)

def pack_forward(rows, seg_pack, weights):
    normed, grouped = mixer_inputs(rows, weights)
    mixed = join_groups(grouped_mixer(*grouped, seg_pack)).astype(jnp.bfloat16)
    return rows + jnp.dot(mixed, weights[11], preferred_element_type=jnp.float32)

def pack_backward(rows, seg_pack, upstream, weights):
    norm_gain, weight_z, weight_x, weight_bc, weight_dt = weights[:5]
    weight_out = weights[11]
    highest = lax.Precision.HIGHEST
    normed, grouped = mixer_inputs(rows, weights)

    def local_mixer(*inputs):
        return grouped_mixer(*inputs, seg_pack)
    mixed, mixer_pull = jax.vjp(local_mixer, *grouped)
    mixed_b = join_groups(mixed).astype(jnp.bfloat16)
    incoming = upstream.astype(jnp.bfloat16)
    grad_mixed = lax.dot_general(incoming, weight_out, contract_cols, preferred_element_type=jnp.float32)
    grad_out = lax.dot_general(mixed_b, incoming, contract_rows, preferred_element_type=jnp.float32)
    pulled = mixer_pull(split_groups(grad_mixed))
    back_z = join_groups(pulled[0]).astype(jnp.bfloat16)
    back_x = join_groups(pulled[1]).astype(jnp.bfloat16)
    back_bc = pulled[2].astype(jnp.bfloat16)
    back_dt = join_groups(pulled[3]).astype(jnp.bfloat16)
    grad_z = lax.dot_general(normed, back_z, contract_rows, preferred_element_type=jnp.float32)
    grad_x = lax.dot_general(normed, back_x, contract_rows, preferred_element_type=jnp.float32)
    grad_dt = lax.dot_general(normed, back_dt, contract_rows, preferred_element_type=jnp.float32)
    grad_bc = jnp.einsum('td,gtc->dc', normed.astype(jnp.float32), back_bc.astype(jnp.float32), precision=highest)
    spread = lax.dot_general(back_z, weight_z, contract_cols, preferred_element_type=jnp.float32) + lax.dot_general(back_x, weight_x, contract_cols, preferred_element_type=jnp.float32) + lax.dot_general(back_dt, weight_dt, contract_cols, preferred_element_type=jnp.float32) + jnp.einsum('gtc,dc->td', back_bc.astype(jnp.float32), weight_bc.astype(jnp.float32), precision=highest)
    _, norm_pull = jax.vjp(rms_norm, rows, norm_gain)
    norm_back, grad_gain = norm_pull(spread)
    grads = (grad_gain, grad_z, grad_x, grad_bc, grad_dt, join_groups(pulled[4]), lax.optimization_barrier(jnp.sum(pulled[5], axis=0)), pulled[6].reshape(-1), pulled[7].reshape(-1), pulled[8].reshape(-1), pulled[9].reshape(-1), grad_out)
    return (upstream + norm_back, grads)

def reference(hidden, seg_ids, norm_gain, weight_z, weight_x, weight_bc, weight_dt, taps_x, taps_bc, dt_bias, decay_log, skip_gain, gate_gain, weight_out, cotangent):
    params = (norm_gain, weight_z, weight_x, weight_bc, weight_dt, taps_x, taps_bc, dt_bias, decay_log, skip_gain, gate_gain, weight_out)
    packs = hidden.shape[0] // TOK_DEV
    seg_packs = seg_ids.reshape(packs, TOK_DEV)
    history = [hidden.reshape(packs, TOK_DEV, D)]
    for layer in range(LAYERS):
        weights = tuple((member[layer] for member in params))

        def forward_step(carry, block):
            return (carry, pack_forward(block[0], block[1], weights))
        _, following = lax.scan(forward_step, None, (history[-1], seg_packs))
        history.append(following)
    upstream = cotangent.reshape(packs, TOK_DEV, D)
    collected = [None] * LAYERS
    for layer in reversed(range(LAYERS)):
        weights = tuple((member[layer] for member in params))
        zeros = tuple((jnp.zeros(member[layer].shape, jnp.float32) for member in params))

        def backward_step(totals, block):
            passed, grads = pack_backward(block[0], block[1], block[2], weights)
            return (tuple((first + second for first, second in zip(totals, grads))), passed)
        totals, upstream = lax.scan(backward_step, zeros, (history[layer], seg_packs, upstream))
        collected[layer] = totals
    stacked = [jnp.stack([collected[layer][member] for layer in range(LAYERS)]) for member in range(12)]
    return (history[-1].reshape(-1, D), upstream.reshape(-1, D), stacked[0], stacked[1], stacked[2], stacked[3], stacked[4], stacked[5], stacked[6], stacked[7], stacked[8], stacked[9], stacked[10], stacked[11])
```

```python
from functools import partial

import jax
import jax.numpy as jnp
from jax import lax
from jax.experimental import pallas as pl
from jax.experimental.pallas import tpu as pltpu
from jax.sharding import PartitionSpec as P

LANES = 128
CHUNK = 32
epsilon = 1e-05
bf16 = jnp.bfloat16
f32 = jnp.float32
HIGHEST = lax.Precision.HIGHEST
ANY = pl.BlockSpec(memory_space=pl.ANY)
VMEM = pl.BlockSpec(memory_space=pltpu.VMEM)
SMEM = pl.BlockSpec(memory_space=pltpu.SMEM)


def nn(a, b, **kw):
    return lax.dot_general(a, b, (((1,), (0,)), ((), ())), preferred_element_type=f32, **kw)


def nt(a, b, **kw):
    return lax.dot_general(a, b, (((1,), (1,)), ((), ())), preferred_element_type=f32, **kw)


def tn(a, b, **kw):
    return lax.dot_general(a, b, (((0,), (0,)), ((), ())), preferred_element_type=f32, **kw)


def sigmoid(v):
    return 1.0 / (1.0 + jnp.exp(-v))


def invoke(kernel, name, outs, smem, vmem, hbm, scratch, flops, nbytes):
    return pl.pallas_call(
        kernel,
        name=name,
        out_shape=[jax.ShapeDtypeStruct(s, d) for s, d, _ in outs],
        in_specs=[SMEM] * len(smem) + [VMEM] * len(vmem) + [ANY] * len(hbm),
        out_specs=[VMEM if on else ANY for _, _, on in outs],
        scratch_shapes=scratch,
        cost_estimate=pl.CostEstimate(flops=flops, bytes_accessed=nbytes, transcendentals=0),
    )(*smem, *vmem, *hbm)


def stages(n):
    core = 2 if n % 2 == 0 else 1
    rest = n // core
    mid = 1
    while rest % (2 * mid) == 0 and 4 * mid * mid <= rest:
        mid *= 2
    return core, mid, rest // mid


def swap(x, axis, n, k):
    return lax.ppermute(x, axis, [(i, i ^ k) for i in range(n)])


def gather_rels(n):
    nc, ny, nz = stages(n)
    return [
        [z * nc * ny + y * nc + c for z in range(nz)] for c in range(nc) for y in range(ny)
    ]


def gather_outer(mine, n):
    nc, ny, nz = stages(n)
    parts = [mine] + [swap(mine, "dp", n, z * nc * ny) for z in range(1, nz)]
    return jnp.concatenate(parts, axis=0)


def gather_rest(outer, n):
    nc, ny, nz = stages(n)
    rows = [outer] + [swap(outer, "dp", n, y * nc) for y in range(1, ny)]
    return rows + [swap(r, "dp", n, c) for c in range(1, nc) for r in rows]


def scatter_rels(n):
    nc, ny, nz = stages(n)
    return [
        [z * nc * ny + y * nc + c for y in range(ny) for z in range(nz)] for c in range(nc)
    ]


def scatter_rest(parts, n):
    nc, ny, nz = stages(n)
    got = [swap(parts[c], "dp", n, c) for c in range(1, nc)]
    size = parts[0].shape[0] // ny
    cols = parts[0].shape[1]

    def block(y, lo, hi):
        total = parts[0][y * size + lo : y * size + hi].astype(f32)
        for g in got:
            total = total + g[y * size + lo : y * size + hi].astype(f32)
        return total

    got_y = [swap(block(y, 0, size).astype(bf16), "dp", n, y * nc) for y in range(1, ny)]
    rows = size // nz

    def summed(z):
        total = block(0, z * rows, (z + 1) * rows)
        for g in got_y:
            total = total + g[z * rows : (z + 1) * rows].astype(f32)
        return total

    got_z = [swap(summed(z).astype(bf16), "dp", n, z * nc * ny) for z in range(1, nz)]
    total = summed(0)
    for g in got_z:
        total = total + g.astype(f32)
    return total


def sum_over(x, axis, n):
    k = 1
    while k < n:
        x = x + swap(x, axis, n, k)
        k *= 2
    return x


def fetch(refs, rels, me, dst, sems):
    copies = []
    for ref, ids in zip(refs, rels):
        rows = ref.shape[0] // len(ids)
        for j, k in enumerate(ids):
            at = pl.multiple_of((me ^ k) * rows, rows)
            c = pltpu.make_async_copy(
                ref.at[pl.ds(j * rows, rows), :],
                dst.at[pl.ds(at, rows), :],
                sems.at[len(copies)],
            )
            c.start()
            copies.append(c)
    return copies


def deliver(src, refs, rels, me, sems):
    copies = []
    for ref, ids in zip(refs, rels):
        rows = ref.shape[0] // len(ids)
        for j, k in enumerate(ids):
            at = pl.multiple_of((me ^ k) * rows, rows)
            c = pltpu.make_async_copy(
                src.at[pl.ds(at, rows), :],
                ref.at[pl.ds(j * rows, rows), :],
                sems.at[len(copies)],
            )
            c.start()
            copies.append(c)
    return copies


def join(parts, t, dst):
    rows = parts[0].shape[0]
    for j, part in enumerate(parts):
        dst[pl.ds(pl.multiple_of((t ^ j) * rows, rows), rows), :] = part[...]


def part(src, t, j, rows):
    return src[pl.ds(pl.multiple_of((t ^ j) * rows, rows), rows), :]


def conv(u, taps, masks):
    last = 3
    total = taps[last + 1 : last + 2, :] + taps[last : last + 1, :] * u
    for k in range(1, last + 1):
        total = total + taps[last - k : last - k + 1, :] * (
            masks[:, k - 1 : k] * pltpu.roll(u, k, 0)
        )
    return total


def conv_back(dpre, u, taps, masks):
    last = 3
    size = dpre.shape[0]
    total = taps[last : last + 1, :] * dpre
    rows = [None] * (last + 2)
    rows[last + 1] = jnp.sum(dpre, axis=0, keepdims=True)
    rows[last] = jnp.sum(dpre * u, axis=0, keepdims=True)
    for k in range(1, last + 1):
        q = pltpu.roll(masks[:, k - 1 : k] * dpre, size - k, 0)
        total = total + taps[last - k : last - k + 1, :] * q
        rows[last - k] = jnp.sum(q * u, axis=0, keepdims=True)
    pad = jnp.zeros((3, dpre.shape[1]), f32)
    return total, jnp.concatenate(rows + [pad], axis=0)


def steps_of(pdt, par):
    a = pdt + par[0:1, :]
    step = jnp.maximum(a, 0.0) + jnp.log1p(jnp.exp(-jnp.abs(a)))
    rate = -step * jnp.exp(par[1:2, :])
    cum = rate
    size = cum.shape[0]
    row = lax.broadcasted_iota(jnp.int32, cum.shape, 0)
    k = 1
    while k < size:
        cum = cum + jnp.where(row >= k, pltpu.roll(cum, k, 0), 0.0)
        k *= 2
    return a, step, rate, cum


def spreader(rows, cols, width):
    r = lax.broadcasted_iota(jnp.int32, (rows, cols), 0) * width
    c = lax.broadcasted_iota(jnp.int32, (rows, cols), 1)
    return jnp.where((c >= r) & (c < r + width), 1.0, 0.0).astype(f32)


def scan_forward(dims, ids, *refs):
    nt_, n, heads, width, states, rels = dims
    parts = refs[:nt_]
    masks, bias, taps, par = refs[nt_ : nt_ + 4]
    wrefs = refs[nt_ + 4 : nt_ + 4 + len(rels)]
    n_ref, proj, y_ref, w, cb, ct, sc, se, sems = refs[nt_ + 4 + len(rels) :]
    copies = fetch(wrefs, rels, ids[0], w, sems)
    join(parts, ids[1], n_ref)
    size = n_ref.shape[0]
    inner = heads * width
    for c in copies:
        c.wait()
    proj[...] = nn(n_ref[...], w[...])
    _, step, _, cum = steps_of(proj[:, inner + 2 * states :], par)
    cum_t = cum.T
    for h in range(heads):
        ct[h] = cum_t[h : h + 1, :]
    cb[...] = nn(cum, spreader(LANES, heads * LANES, LANES), precision=HIGHEST)
    se[...] = nn(step, spreader(LANES, inner, width), precision=HIGHEST)
    pre = conv(proj[:, inner : inner + 2 * states], taps[:, inner:], masks)
    bc = pre * sigmoid(pre)
    sc[...] = nt(bc[:, states:], bc[:, :states], precision=HIGHEST)
    skip = nn(par[...], spreader(LANES, inner, width), precision=HIGHEST)
    per = LANES // width
    lane = lax.broadcasted_iota(jnp.int32, (LANES, LANES), 1)

    y_ref[0:8, :] = skip

    skip_row = y_ref[2:3, :]
    y_ref[...] = jnp.broadcast_to(skip_row, y_ref.shape)

    def body(p, carry):
        at = pl.ds(pl.multiple_of(p * LANES, LANES), LANES)
        pre = conv(proj[:, at], taps[:, at], masks)
        v = pre * sigmoid(pre)
        u = (v * se[:, at]).astype(bf16)
        for rb in range(size // LANES):
            r0 = rb * LANES
            cols = r0 + LANES
            out = None
            for h in range(per):
                head = p * per + h
                col = cb[r0:cols, pl.ds(pl.multiple_of(head * LANES, LANES), LANES)]
                row = ct[head, :, 0:cols]
                gap = jnp.concatenate([col] * (rb + 1), axis=1) - row + bias[r0:cols, 0:cols]
                g = jnp.exp(gap) * sc[r0:cols, 0:cols]
                o = nn(g.astype(bf16), u[0:cols])
                out = o if out is None else jnp.where(lane >= h * width, o, out)
            y_ref[r0:cols, at] = y_ref[r0:cols, at] * v[r0:cols] + out
        return carry

    lax.fori_loop(0, inner // LANES, body, 0)


def gate_forward(dims, ids, n_ref, y_ref, gain, *refs):
    nt_, n, rels = dims
    wrefs = refs[: len(rels)]
    refs = refs[len(rels) :]
    pz, mixed, keep = refs[:3]
    sends = refs[3 : 2 + nt_]
    w, out, sems = refs[2 + nt_ :]
    copies = fetch(wrefs, rels, ids[0], w, sems)
    inner = y_ref.shape[1]
    size = y_ref.shape[0]
    for c in copies:
        c.wait()
    pz[...] = nn(n_ref[...], w[:, :inner])

    def body(i, carry):
        at = pl.ds(pl.multiple_of(i * CHUNK, CHUNK), CHUNK)
        z = pz[at, :]
        g = y_ref[at, :] * (z * sigmoid(z))
        r = lax.rsqrt(jnp.mean(g * g, axis=1, keepdims=True) + epsilon)
        mixed[at, :] = (g * r * gain[...]).astype(bf16)
        return carry

    lax.fori_loop(0, size // CHUNK, body, 0)
    out[...] = nt(mixed[...], w[:, inner:])
    rows = keep.shape[0]
    keep[...] = part(out, ids[1], 0, rows)
    for j in range(1, nt_):
        sends[j - 1][...] = part(out, ids[1], j, rows).astype(bf16)


def norm_first(h, gain, normed):
    x = h[...]
    r = lax.rsqrt(jnp.mean(x * x, axis=1, keepdims=True) + epsilon)
    normed[...] = (x * r * gain[...]).astype(bf16)


def norm_next(h, gain, keep, *refs):
    recvs, (h_out, normed) = refs[:-2], refs[-2:]
    x = keep[...]
    for r in recvs:
        x = x + r[...].astype(f32)
    x = h[...] + x
    h_out[...] = x
    r = lax.rsqrt(jnp.mean(x * x, axis=1, keepdims=True) + epsilon)
    normed[...] = (x * r * gain[...]).astype(bf16)


def norm_back(h, gain, up, keep, *refs):
    recvs, (up_out, up_b, dgain) = refs[:-3], refs[-3:]
    d = keep[...]
    for r in recvs:
        d = d + r[...].astype(f32)
    x = h[...]
    r = lax.rsqrt(jnp.mean(x * x, axis=1, keepdims=True) + epsilon)
    dgain[...] = jnp.broadcast_to(jnp.sum(d * x * r, axis=0, keepdims=True), dgain.shape)
    d = d * gain[...]
    back = d * r - x * (r * r * r * jnp.mean(d * x, axis=1, keepdims=True))
    e = up[...] + back
    up_out[...] = e
    up_b[...] = e.astype(bf16)


def gate_backward(dims, ids, *refs):
    nt_, n, rels, outs_rels = dims
    parts = refs[:nt_]
    n_ref, y_ref, pz, mixed, gain = refs[nt_ : nt_ + 5]
    wrefs = refs[nt_ + 5 : nt_ + 5 + len(rels)]
    refs = refs[nt_ + 5 + len(rels) :]
    dy, spread, dgain = refs[:3]
    grads = refs[3 : 3 + len(outs_rels)]
    w, up, bz, g_all, sems = refs[3 + len(outs_rels) :]
    copies = fetch(wrefs, rels, ids[0], w, sems)
    join(parts, ids[1], up)
    size, inner = y_ref.shape
    depth = n_ref.shape[1]
    for c in copies:
        c.wait()
    dy[...] = nn(up[...], w[:, inner:])
    dgain[...] = jnp.zeros_like(dgain)

    def body(i, carry):
        at = pl.ds(pl.multiple_of(i * CHUNK, CHUNK), CHUNK)
        z = pz[at, :]
        s = sigmoid(z)
        zs = z * s
        y = y_ref[at, :]
        g = y * zs
        r = lax.rsqrt(jnp.mean(g * g, axis=1, keepdims=True) + epsilon)
        d = dy[at, :]
        dg = d * g * r
        dgain[...] += jnp.sum(dg.reshape(CHUNK // 8, 8, inner), axis=0)
        d = d * gain[...]
        d = d * r - g * (r * r * r * jnp.mean(d * g, axis=1, keepdims=True))
        dy[at, :] = d * zs
        bz[at, :] = (d * y * (s + zs * (1.0 - s))).astype(bf16)
        return carry

    lax.fori_loop(0, size // CHUNK, body, 0)
    step = 256
    for r0 in range(0, depth, step):
        g_all[r0 : r0 + step, :inner] = tn(n_ref[:, r0 : r0 + step], bz[...]).astype(bf16)
        g_all[r0 : r0 + step, inner:] = tn(up[:, r0 : r0 + step], mixed[...]).astype(bf16)
    copies = deliver(g_all, grads, outs_rels, ids[0], sems)
    spread[...] = nt(bz[...], w[:, :inner])
    for c in copies:
        c.wait()


def scan_backward(dims, ids, *refs):
    nt_, n, heads, width, states, rels = dims
    dy, proj, spread, masks, bias, taps, par = refs[:7]
    wrefs = refs[7 : 7 + len(rels)]
    refs = refs[7 + len(rels) :]
    back, dtaps, dpar, keep = refs[:4]
    sends = refs[4 : 3 + nt_]
    w, cb, ct, sc, se, sk, ds, du_v, dy_v, dc, cs, out, sems = refs[3 + nt_ :]
    copies = fetch(wrefs, rels, ids[0], w, sems)
    size = proj.shape[0]
    inner = heads * width
    a, step, rate, cum = steps_of(proj[:, inner + 2 * states :], par)
    cum_t = cum.T
    for h in range(heads):
        ct[h] = cum_t[h : h + 1, :]
    cb[...] = nn(cum, spreader(LANES, heads * LANES, LANES), precision=HIGHEST)
    se[...] = nn(step, spreader(LANES, inner, width), precision=HIGHEST)
    sk[...] = nn(par[...], spreader(LANES, inner, width), precision=HIGHEST)
    ubc = proj[:, inner : inner + 2 * states]
    pre_bc = conv(ubc, taps[:, inner:], masks)
    sig_bc = sigmoid(pre_bc)
    bc = pre_bc * sig_bc
    sc[...] = nt(bc[:, states:], bc[:, :states], precision=HIGHEST)
    ds[...] = jnp.zeros_like(ds)
    dc[...] = jnp.zeros_like(dc)
    per = LANES // width
    nb = size // LANES
    lane = lax.broadcasted_iota(jnp.int32, (LANES, LANES), 1)

    def body(p, carry):
        at = pl.ds(pl.multiple_of(p * LANES, LANES), LANES)
        ux = proj[:, at]
        pre = conv(ux, taps[:, at], masks)
        sig = sigmoid(pre)
        v = pre * sig
        stepx = se[:, at]
        u = (v * stepx).astype(bf16)
        dyp = dy[:, at]
        dyb = dyp.astype(bf16)
        du = [None] * nb
        for h in range(per):
            head = p * per + h
            colsum = [None] * nb
            gs = []
            for rb in range(nb):
                r0 = rb * LANES
                cols = r0 + LANES
                col = cb[r0:cols, pl.ds(pl.multiple_of(head * LANES, LANES), LANES)]
                row = ct[head, :, 0:cols]
                gap = jnp.concatenate([col] * (rb + 1), axis=1) - row + bias[r0:cols, 0:cols]
                l = jnp.exp(gap)
                g = l * sc[r0:cols, 0:cols]
                gs.append(g.astype(bf16))
                dym = jnp.where(
                    (lane >= h * width) & (lane < (h + 1) * width), dyp[r0:cols], 0.0
                ).astype(bf16)
                dp = nt(dym, u[0:cols])
                ds[r0:cols, 0:cols] += dp * l
                m = dp * g
                rs = jnp.sum(m, axis=1, keepdims=True)
                dc[r0:cols, :] += jnp.where(lane == head, rs, 0.0)
                c = jnp.sum(m, axis=0, keepdims=True)
                for sb in range(rb + 1):
                    piece = c[:, sb * LANES : (sb + 1) * LANES]
                    colsum[sb] = piece if colsum[sb] is None else colsum[sb] + piece
            cs[head] = jnp.concatenate(colsum, axis=1)
            for sb in range(nb):
                s0 = sb * LANES
                g = jnp.concatenate([x[:, s0 : s0 + LANES] for x in gs[sb:]], axis=0)
                o = tn(g, dyb[s0:])
                du[sb] = o if du[sb] is None else jnp.where(lane >= h * width, o, du[sb])
        du = jnp.concatenate(du, axis=0)
        du_v[:, at] = du * v
        dy_v[:, at] = jnp.broadcast_to(jnp.sum(dyp * v, axis=0, keepdims=True), (8, LANES))
        dv = sk[2:3, at] * dyp + du * stepx
        dpre = dv * (sig + v * (1.0 - sig))
        dx, rows = conv_back(dpre, ux, taps[:, at], masks)
        back[:, at] = dx.astype(bf16)
        dtaps[:, at] = rows
        return carry

    lax.fori_loop(0, inner // LANES, body, 0)
    dcc = nn(ds[...], bc[:, :states], precision=HIGHEST)
    dbb = nn(ds[...].T, bc[:, states:], precision=HIGHEST)
    dbc = jnp.concatenate([dbb, dcc], axis=1)
    dpre = dbc * (sig_bc + bc * (1.0 - sig_bc))
    dx, rows = conv_back(dpre, ubc, taps[:, inner:], masks)
    back[:, inner : inner + 2 * states] = dx.astype(bf16)
    dtaps[:, inner:] = rows
    sums = jnp.concatenate(
        [cs[h] for h in range(heads)] + [jnp.zeros((LANES - heads, size), f32)], axis=0
    )
    drate = dc[...] - sums.T
    row = lax.broadcasted_iota(jnp.int32, drate.shape, 0)
    k = 1
    while k < size:
        drate = drate + jnp.where(row < size - k, pltpu.roll(drate, size - k, 0), 0.0)
        k *= 2
    gather = spreader(LANES, inner, width)
    dstep = nt(du_v[...], gather, precision=HIGHEST) - drate * jnp.exp(par[1:2, :])
    da = dstep * sigmoid(a)
    back[:, inner + 2 * states :] = da.astype(bf16)
    dskip = nt(dy_v[...], gather, precision=HIGHEST)
    dpar[...] = jnp.concatenate(
        [
            jnp.sum(da, axis=0, keepdims=True),
            jnp.sum(drate * rate, axis=0, keepdims=True),
            dskip[0:6, :],
        ],
        axis=0,
    )
    for c in copies:
        c.wait()
    out[...] = spread[...] + nt(back[...], w[...])
    rows = keep.shape[0]
    keep[...] = part(out, ids[1], 0, rows)
    for j in range(1, nt_):
        sends[j - 1][...] = part(out, ids[1], j, rows).astype(bf16)


def weight_backward(dims, ids, n_ref, back, *refs):
    (outs_rels,) = dims
    grads = refs[: len(outs_rels)]
    g_all, sems = refs[len(outs_rels) :]
    step = 256
    for r0 in range(0, n_ref.shape[1], step):
        g_all[r0 : r0 + step, :] = tn(n_ref[:, r0 : r0 + step], back[...]).astype(bf16)
    for c in deliver(g_all, grads, outs_rels, ids[0], sems):
        c.wait()


def local(
    n,
    m,
    hidden,
    seg_ids,
    norm_gain,
    weight_z,
    weight_x,
    weight_bc,
    weight_dt,
    taps_x,
    taps_bc,
    dt_bias,
    decay_log,
    skip_gain,
    gate_gain,
    weight_out,
    cotangent,
):
    layers, share, inner = weight_z.shape
    rows, depth = hidden.shape
    size = seg_ids.shape[0]
    heads = dt_bias.shape[1]
    width = inner // heads
    states = weight_bc.shape[2] // 2
    wide = inner + 2 * states + LANES
    pair = 2 * inner
    ids = jnp.stack([lax.axis_index("dp"), lax.axis_index("tensor")]).astype(jnp.int32)
    rels = gather_rels(n)
    out_rels = scatter_rels(n)
    dma = pltpu.SemaphoreType.DMA((n,))

    position = jnp.arange(size)
    masks = jnp.stack(
        [
            ((position >= k) & (jnp.roll(seg_ids, k) == seg_ids)).astype(f32)
            for k in range(1, 9)
        ],
        axis=1,
    )
    bias = jnp.where(
        (seg_ids[:, None] == seg_ids[None, :]) & (position[:, None] >= position[None, :]),
        0.0,
        -1e30,
    ).astype(f32)
    taps = jnp.pad(jnp.concatenate([taps_x, taps_bc], axis=2), ((0, 0), (0, 3), (0, 0)))
    par = jnp.pad(
        jnp.stack([dt_bias, decay_log, skip_gain], axis=1),
        ((0, 0), (0, 5), (0, LANES - heads)),
    )

    bc_rows = lax.all_gather(weight_bc, "tensor", axis=1, tiled=True)
    xs = [
        jnp.concatenate(
            [
                weight_x[l],
                bc_rows[l],
                jnp.pad(weight_dt[l], ((0, 0), (0, LANES - heads))),
            ],
            axis=1,
        )
        for l in range(layers)
    ]
    zs = [jnp.concatenate([weight_z[l], weight_out[l].T], axis=1) for l in range(layers)]
    wx, wz = [None] * layers, [None] * layers
    last = None
    for l in range(layers):
        for store, mine in ((wx, xs[l]), (wz, zs[l])):
            if last is not None:
                mine, last = lax.optimization_barrier((mine, last))
            last = gather_outer(mine, n)
            store[l] = gather_rest(last, n)

    def exchange(sends):
        return [swap(s, "tensor", m, j + 1) for j, s in enumerate(sends)]

    gains = [norm_gain[l][None, :] for l in range(layers)]
    gates = [gate_gain[l][None, :] for l in range(layers)]
    h = hidden
    (normed,) = invoke(
        norm_first, "norm_first", [((rows, depth), bf16, True)], [], [h, gains[0]], [], [],
        10 * rows * depth, 6 * rows * depth,
    )
    up_parts = None
    saved = []
    for l in range(layers):
        parts = [normed] + exchange([normed] * (m - 1))
        full, proj, y = invoke(
            partial(scan_forward, (m, n, heads, width, states, rels)),
            "scan_forward",
            [((size, depth), bf16, True), ((size, wide), f32, True), ((size, inner), f32, True)],
            [ids],
            parts + [masks, bias, taps[l], par[l]],
            wx[l],
            [
                pltpu.VMEM((depth, wide), bf16),
                pltpu.VMEM((size, heads * LANES), f32),
                pltpu.VMEM((heads, 1, size), f32),
                pltpu.VMEM((size, size), f32),
                pltpu.VMEM((size, inner), f32),
                dma,
            ],
            2 * size * depth * wide,
            2 * depth * wide + 4 * size * (wide + inner),
        )
        res = invoke(
            partial(gate_forward, (m, n, rels)),
            "gate_forward",
            [((size, inner), f32, True), ((size, inner), bf16, True), ((rows, depth), f32, True)]
            + [((rows, depth), bf16, True)] * (m - 1),
            [ids],
            [full, y, gates[l]],
            wz[l],
            [pltpu.VMEM((depth, pair), bf16), pltpu.VMEM((size, depth), f32), dma],
            2 * size * depth * pair,
            2 * depth * pair + 8 * size * inner,
        )
        pz, mixed, keep = res[:3]
        recvs = exchange(res[3:])
        saved.append((h, full, proj, y, pz, mixed))
        if l + 1 < layers:
            h, normed = invoke(
                norm_next, "norm_next", [((rows, depth), f32, True), ((rows, depth), bf16, True)],
                [], [h, gains[l + 1], keep] + recvs, [], [],
                10 * rows * depth, 16 * rows * depth,
            )
        else:
            total = keep
            for r in recvs:
                total = total + r.astype(f32)
            block_out = h + total
    up = cotangent
    up_b = cotangent.astype(bf16)
    grads_z, grads_x = [None] * layers, [None] * layers
    small, gain_terms = [None] * layers, [None] * layers
    for l in reversed(range(layers)):
        h, full, proj, y, pz, mixed = saved[l]
        parts = [up_b] + exchange([up_b] * (m - 1))
        res = invoke(
            partial(gate_backward, (m, n, rels, out_rels)),
            "gate_backward",
            [((size, inner), f32, True), ((size, depth), f32, True), ((8, inner), f32, True)]
            + [((share * len(r), pair), bf16, False) for r in out_rels],
            [ids],
            parts + [full, y, pz, mixed, gates[l]],
            wz[l],
            [
                pltpu.VMEM((depth, pair), bf16),
                pltpu.VMEM((size, depth), bf16),
                pltpu.VMEM((size, inner), bf16),
                pltpu.VMEM((depth, pair), bf16),
                dma,
            ],
            4 * size * depth * pair,
            4 * depth * pair + 16 * size * inner,
        )
        dy, spread, dgate = res[:3]
        grads_z[l] = scatter_rest(res[3:], n)
        res = invoke(
            partial(scan_backward, (m, n, heads, width, states, rels)),
            "scan_backward",
            [
                ((size, wide), bf16, True),
                ((8, inner + 2 * states), f32, True),
                ((8, LANES), f32, True),
                ((rows, depth), f32, True),
            ]
            + [((rows, depth), bf16, True)] * (m - 1),
            [ids],
            [dy, proj, spread, masks, bias, taps[l], par[l]],
            wx[l],
            [
                pltpu.VMEM((depth, wide), bf16),
                pltpu.VMEM((size, heads * LANES), f32),
                pltpu.VMEM((heads, 1, size), f32),
                pltpu.VMEM((size, size), f32),
                pltpu.VMEM((size, inner), f32),
                pltpu.VMEM((8, inner), f32),
                pltpu.VMEM((size, size), f32),
                pltpu.VMEM((size, inner), f32),
                pltpu.VMEM((8, inner), f32),
                pltpu.VMEM((size, LANES), f32),
                pltpu.VMEM((heads, 1, size), f32),
                pltpu.VMEM((size, depth), f32),
                dma,
            ],
            6 * size * depth * wide,
            4 * depth * wide + 16 * size * inner,
        )
        back, dtaps, dpar, keep = res[:4]
        recvs = exchange(res[4:])
        grad = invoke(
            partial(weight_backward, (out_rels,)),
            "weight_backward",
            [((share * len(r), wide), bf16, False) for r in out_rels],
            [ids],
            [full, back],
            [],
            [pltpu.VMEM((depth, wide), bf16), dma],
            2 * size * depth * wide,
            2 * depth * wide,
        )
        grads_x[l] = scatter_rest(grad, n)
        up, up_b, dgain = invoke(
            norm_back, "norm_back",
            [((rows, depth), f32, True), ((rows, depth), bf16, True), ((8, depth), f32, True)],
            [], [h, gains[l], up, keep] + recvs, [], [],
            20 * rows * depth, 20 * rows * depth,
        )
        small[l] = (dtaps, dpar, jnp.sum(dgate, axis=0))
        gain_terms[l] = dgain[0]

    def over_dp(x):
        return sum_over(x, "dp", n)

    sizes = [8 * (inner + 2 * states), 8 * LANES, inner]
    flat = jnp.concatenate(
        [piece.reshape(-1) for l in range(layers) for piece in small[l]]
    ).reshape(-1, LANES)
    flat = over_dp(flat).reshape(-1)
    outs = []
    at = 0
    for l in range(layers):
        row = []
        for s in sizes:
            row.append(flat[at : at + s])
            at += s
        outs.append(row)
    taps_sum = jnp.stack([o[0].reshape(8, -1) for o in outs])
    par_sum = jnp.stack([o[1].reshape(8, LANES) for o in outs])
    gate_sum = jnp.stack([o[2] for o in outs])
    grad_norm_gain = sum_over(over_dp(jnp.stack(gain_terms)), "tensor", m)
    grad_taps_bc = sum_over(taps_sum[:, :5, inner:], "tensor", m)

    t = ids[1]
    part_rows = share // m
    bcs = []
    for l in range(layers):
        g = grads_x[l][:, inner : inner + 2 * states]
        total = lax.dynamic_slice_in_dim(g, t * part_rows, part_rows, 0)
        for j in range(1, m):
            piece = lax.dynamic_slice_in_dim(g, (t ^ j) * part_rows, part_rows, 0)
            total = total + swap(piece, "tensor", m, j)
        bcs.append(total)
    return (
        block_out,
        up,
        grad_norm_gain,
        jnp.stack([g[:, :inner] for g in grads_z]),
        jnp.stack([g[:, :inner] for g in grads_x]),
        jnp.stack(bcs),
        jnp.stack([g[:, inner + 2 * states : inner + 2 * states + heads] for g in grads_x]),
        taps_sum[:, :5, :inner],
        grad_taps_bc,
        par_sum[:, 0, :heads],
        par_sum[:, 1, :heads],
        par_sum[:, 2, :heads],
        gate_sum,
        jnp.stack([g[:, inner:].T for g in grads_z]),
    )


def solution(mesh):
    return jax.shard_map(
        partial(local, mesh.shape["dp"], mesh.shape["tensor"]),
        mesh=mesh,
        in_specs=(
            P(("dp", "tensor"), None),
            P("dp"),
            P(),
            P(None, "dp", "tensor"),
            P(None, "dp", "tensor"),
            P(None, ("dp", "tensor"), None),
            P(None, "dp", "tensor"),
            P(None, None, "tensor"),
            P(),
            P(None, "tensor"),
            P(None, "tensor"),
            P(None, "tensor"),
            P(None, "tensor"),
            P(None, "tensor", "dp"),
            P(("dp", "tensor"), None),
        ),
        out_specs=(
            P(("dp", "tensor"), None),
            P(("dp", "tensor"), None),
            P(),
            P(None, "dp", "tensor"),
            P(None, "dp", "tensor"),
            P(None, ("dp", "tensor"), None),
            P(None, "dp", "tensor"),
            P(None, None, "tensor"),
            P(),
            P(None, "tensor"),
            P(None, "tensor"),
            P(None, "tensor"),
            P(None, "tensor"),
            P(None, "tensor", "dp"),
        ),
        check_vma=False,
    )
```
